32 devices in a mesh: row: 4 (over y, core), col: 8 (over z, x).
Axes of the slice: x: 2, y: 2, z: 4, core: 2. Of those that a mesh axis runs over, the one named last changes fastest.
Arguments:
- schur_matrix: float32 [16384, 16384], P('row', 'col'), may hold values from -3 to 7
- newton_rhs: float32 [16384], P('row'), may hold values from -6 to 6
Outputs:
- reduced_matrix: float32 [16384, 16384], P('row', 'col')
- reduced_rhs: float32 [16384], P('row')
The draws below stay inside these ranges and needn't reach their ends.
All inputs are finite; a program needn't handle non-finite values.
Results may differ from the reference program's by a relative error of at most 0.0001.
Values sent between devices are 32-bit elements; how exact they have to be, the bound alone decides.
No kernel may reach another device: no remote copies, remote signals or barrier semaphores. Data moves between devices by JAX's collectives and lax.ppermute only.
A program may use at most 128 MiB of HBM per device.

```python
import jax
import jax.numpy as jnp
from jax import lax

N = 16384
NB = 512
SECTIONS = 1
N_ROW = 4
N_COL = 8


def natural_index(count, axis_count):
    stored = jnp.arange(count, dtype=jnp.int32)
    local = count // axis_count
    device = stored // local
    within = stored % local
    block = within // NB * axis_count + device
    return block * NB + within % NB


def draw_schur_matrix(key, part):
    base = jax.random.fold_in(key, 11)
    key_off, key_diag = jax.random.split(base)
    pivot_spread = 0.5 / jnp.sqrt(jnp.float32(NB))
    panel_spread = 1.5 / jnp.sqrt(jnp.sqrt(jnp.float32(NB)))
    coupling = jnp.clip(jax.random.normal(key_off, (N, N), jnp.float32), -4.0, 4.0)
    diag_vals = jnp.exp(jax.random.uniform(key_diag, (N,), jnp.float32, jnp.log(2.0), jnp.log(6.0)))
    nat_rows = natural_index(N, N_ROW)
    nat_cols = natural_index(N, N_COL)
    lead_rows = nat_rows < SECTIONS * NB
    lead_cols = nat_cols < SECTIONS * NB
    scale = jnp.where(lead_rows[:, None] != lead_cols[None, :], panel_spread, pivot_spread)
    on_diag = nat_rows[:, None] == nat_cols[None, :]
    row_diag = diag_vals[nat_rows]
    return coupling * scale + jnp.where(on_diag, row_diag[:, None], 0.0)


def steps_of(stream_key, extent, cuts, least, high):
    def one(axis_at, parts):
        draws = jax.random.uniform(jax.random.fold_in(jax.random.fold_in(stream_key, 6), axis_at), (parts,), jnp.float32, least / len(cuts), high / len(cuts))
        return jnp.repeat(jnp.exp(draws), extent[axis_at] // parts).reshape((-1,) + (1,) * (len(extent) - axis_at - 1))

    gain = one(*cuts[0])
    for cut in cuts[1:]:
        gain = gain * one(*cut)
    return gain


def scatter_about(rng, extent, spread, bound, shards=(), kind=jnp.bfloat16):
    loudness = steps_of(rng, extent, shards, -0.22, 0.18) if shards else 1.0
    result = jax.random.normal(rng, extent, jnp.float32) * spread * loudness
    return jnp.minimum(jnp.maximum(result, -bound), bound).astype(kind)


def setup_inputs(seed: int = 0) -> dict:
    key_list = jax.random.split(jax.random.key(seed), 3)
    schur_matrix = draw_schur_matrix(jax.random.fold_in(key_list[2], 71), 0)
    newton_rhs = scatter_about(key_list[1], (N,), 1.0, 6.0, ((0, 4),), jnp.float32)
    return {"schur_matrix": schur_matrix, "newton_rhs": newton_rhs}


def precise_dot(left, right):
    return jnp.dot(left, right, precision=lax.Precision.HIGHEST, preferred_element_type=jnp.float32)


def newton_inverse(pivot_block):
    identity = jnp.eye(pivot_block.shape[0], dtype=jnp.float32)
    inv_diag = 1.0 / jnp.diagonal(pivot_block)
    first_iter = inv_diag[:, None] * (2.0 * identity - pivot_block * inv_diag[None, :])
    return precise_dot(first_iter, 2.0 * identity - precise_dot(pivot_block, first_iter))


def rows_natural(stored):
    return stored.reshape(N_ROW, N // (N_ROW * NB), NB, -1).transpose(1, 0, 2, 3).reshape(N, -1)


def rows_stored(natural):
    return natural.reshape(N // (N_ROW * NB), N_ROW, NB, -1).transpose(1, 0, 2, 3).reshape(N, -1)


def cols_natural(stored):
    return stored.reshape(N, N_COL, N // (N_COL * NB), NB).transpose(0, 2, 1, 3).reshape(N, N)


def cols_stored(natural):
    return natural.reshape(N, N // (N_COL * NB), N_COL, NB).transpose(0, 2, 1, 3).reshape(N, N)


def reference(schur_matrix, newton_rhs):
    system = cols_natural(rows_natural(schur_matrix))
    vector = rows_natural(newton_rhs[:, None])[:, 0]
    for section_num in range(SECTIONS):
        low = section_num * NB
        high = low + NB
        inverse = newton_inverse(system[low:high, low:high])
        product = precise_dot(inverse, system[low:high, high:])
        solved = precise_dot(inverse, vector[low:high])
        col_panel = system[high:, low:high]
        system = system.at[high:, high:].add(-precise_dot(col_panel, product))
        vector = vector.at[high:].add(-precise_dot(col_panel, solved))
    reduced_matrix = rows_stored(cols_stored(system))
    reduced_rhs = rows_stored(vector[:, None])[:, 0]
    return reduced_matrix, reduced_rhs
```

```python
import jax
import jax.numpy as jnp
from jax import lax
from jax.experimental import pallas as pl
from jax.experimental.pallas import tpu as pltpu
from jax.sharding import PartitionSpec as P


NB = 512
F32, BF16 = jnp.float32, jnp.bfloat16
ANY = pl.BlockSpec(memory_space=pl.ANY)
VMEM = pl.BlockSpec(memory_space=pltpu.VMEM)


def barrier(value, ties):
    return lax.optimization_barrier((value, *ties))[0] if ties else value


def dot(left, right):
    return jnp.dot(left, right, preferred_element_type=F32)


def precise_dot(left, right, dims=(((1,), (0,)), ((), ()))):
    return lax.dot_general(left, right, dims, precision=lax.Precision.HIGHEST, preferred_element_type=F32)


def split_dot(left, right):
    return dot(left[0], right[0]) + dot(left[0], right[1]) + dot(left[1], right[0])


def halves(value):
    high = value.astype(BF16)
    return high, (value - high.astype(F32)).astype(BF16)


def solve_kernel(place, pivot_ref, matrix, *refs):
    *received, high_ref, low_ref, solved_ref, strip, sem = refs
    nb, local_cols = strip.shape
    sources = [matrix.at[:nb, :], *received]
    for at, source in enumerate(sources):

        @pl.when(place[0] == at)
        def _():
            pltpu.make_async_copy(source, strip, sem).start()

    block = pivot_ref[:nb, :]
    on_diag = lax.broadcasted_iota(jnp.int32, (nb, nb), 0) == lax.broadcasted_iota(jnp.int32, (nb, nb), 1)
    diag = jnp.where(on_diag, block, 0.0)
    inv_row = 1.0 / jnp.sum(diag, axis=0, keepdims=True)
    inv_col = 1.0 / jnp.sum(diag, axis=1, keepdims=True)
    twice = jnp.where(on_diag, 2.0, 0.0)
    first_iter = inv_col * (twice - block * inv_row)
    inverse = split_dot(halves(first_iter), halves(twice - split_dot(halves(block), halves(first_iter))))
    solved_ref[...] = precise_dot(pivot_ref[nb:, :], inverse, (((1,), (1,)), ((), ())))
    inv_parts = halves(inverse)
    pltpu.make_async_copy(sources[0], strip, sem).wait()

    @pl.loop(0, local_cols // nb)
    def _(at):
        cols = pl.ds(pl.multiple_of(at * nb, nb), nb)
        product = split_dot(inv_parts, halves(strip[:, cols]))
        product = jnp.where((place[1] == 0) & (at == 0), 0.0, product)
        high_ref[:, cols], low_ref[:, cols] = halves(product)


def update_kernel(count, tile, rhs, high_ref, low_ref, solved_ref, *refs):
    sources = refs[:count]
    out_tile, out_rhs, panel, sems = refs[-4:]
    nb = panel.shape[1]
    at = pl.program_id(0)
    slot = lax.rem(at, 2)

    def fetch(step):
        for which, source in enumerate(sources):

            @pl.when(step == which)
            def _():
                pltpu.make_async_copy(source, panel.at[which % 2], sems.at[which % 2]).start()

    @pl.when(at == 0)
    def _():
        fetch(0)

    pltpu.make_async_copy(sources[0], panel.at[slot], sems.at[slot]).wait()
    fetch(at + 1)
    value = panel[slot]
    out_tile[...] = tile[...] - split_dot(halves(value), (high_ref[...], low_ref[...]))
    terms = value * solved_ref[0:1, :]
    folded = terms[:, :128]
    for low_col in range(128, nb, 128):
        folded = folded + terms[:, low_col : low_col + 128]
    out_rhs[...] = rhs[...] - jnp.sum(folded.T, axis=0, keepdims=True)


def solve(place, pivot, matrix, received):
    local_cols = matrix.shape[1]
    nb = pivot.shape[1]
    return pl.pallas_call(
        solve_kernel,
        grid_spec=pltpu.PrefetchScalarGridSpec(
            num_scalar_prefetch=1,
            grid=(),
            in_specs=[VMEM, ANY, *[ANY] * len(received)],
            out_specs=[VMEM] * 3,
            scratch_shapes=[pltpu.VMEM((nb, local_cols), F32), pltpu.SemaphoreType.DMA],
        ),
        out_shape=[jax.ShapeDtypeStruct((nb, local_cols), BF16)] * 2 + [jax.ShapeDtypeStruct((8, nb), F32)],
        compiler_params=pltpu.CompilerParams(vmem_limit_bytes=24 * 2**20),
        cost_estimate=pl.CostEstimate(flops=6 * nb * nb * local_cols + 24 * nb**3, bytes_accessed=8 * nb * local_cols, transcendentals=0),
        name="solve",
    )(place, pivot, matrix, *received)


def update(start, matrix, rhs, factors, panels, before):
    _, local_cols = matrix.shape
    nb, count = factors[0].shape[0], len(panels)
    at_tile = pl.BlockSpec((nb, local_cols), lambda at: (start + at, 0))
    at_rhs = pl.BlockSpec((1, nb), lambda at: (0, start + at))
    factor = pl.BlockSpec((nb, local_cols), lambda at: (0, 0), pipeline_mode=pl.Buffered(1))
    operands = [matrix, rhs, *factors, *panels, *before]
    return pl.pallas_call(
        lambda *refs: update_kernel(count, *refs),
        grid=(count,),
        in_specs=[at_tile, at_rhs, factor, factor, VMEM, *[ANY] * (count + len(before))],
        out_specs=[at_tile, at_rhs],
        scratch_shapes=[pltpu.VMEM((2, nb, nb), F32), pltpu.SemaphoreType.DMA((2,))],
        out_shape=[jax.ShapeDtypeStruct(matrix.shape, F32), jax.ShapeDtypeStruct(rhs.shape, F32)],
        input_output_aliases={len(operands) - 2 + at: at for at in range(len(before))},
        compiler_params=pltpu.CompilerParams(dimension_semantics=("arbitrary",), vmem_limit_bytes=32 * 2**20),
        cost_estimate=pl.CostEstimate(flops=6 * count * nb * nb * local_cols, bytes_accessed=8 * count * nb * local_cols, transcendentals=0),
        name="update",
    )(*operands)


def fan_out(source, low, high):
    if low >= high:
        return []
    mid = (low + high) // 2
    return [(0, source, mid)] + [(at + 1, a, b) for at, a, b in fan_out(mid, low, mid) + fan_out(mid, mid + 1, high)]


def parent(row):
    return row & (row - 1)


def plan(count, stages, row_count):
    last = max(at for at, _, _ in stages)
    levels = {row: bin(row).count("1") for row in range(1, row_count)}
    late = max(levels.values())
    launches = [(name, at) for at in range(count) for name in ("first", "lower")]
    order = launches[:8] + [("onward", 0)]
    launches = launches[8:]
    side_work = {0: [("strip", row) for row in levels if levels[row] == 1]}
    for level in range(1, late + 1):
        side_work[last + 2 * level] = [(name, row) for name in ("strip", "pivot") for row in levels if levels[row] == level and (name == "pivot" or level > 1)]
    side_work.setdefault(max(count - 1, last + 2 * late + 1), []).append(("solve", 0))
    early = [max(count - 6, 0), max(count - 2, 0)]
    for step in range(count + last + 2):
        for stage in range(1, last + 1):
            pair = step - stage + 1
            if 0 <= pair <= count:
                order += [("spread", pair, b) for s, _, b in stages if s == stage]
        if 0 <= step - last <= count:
            order.append(("cross", step - last))
        if 0 <= step - last - 1 < count:
            order.append(("close", step - last - 1))
        if step + 1 < count:
            order.append(("onward", step + 1))
        if step > 0:
            order += launches[:4]
            launches = launches[4:]
        order += side_work.pop(step, [])
        if step >= count and ("solve", 0) in order and early:
            order.append(("update", early.pop(0)))
    order += launches + [work for at in sorted(side_work) for work in side_work[at]]
    starts = [0, *[step[1] for step in order if step[0] == "update"], count]
    groups = list(zip(sorted({*starts}), sorted({*starts})[1:]))
    ended = {high: low for low, high in groups}
    order = [("update", ended[step[1]], step[1]) if step[0] == "update" else step for step in order if step[0] != "update" or step[1] in ended]
    return order + [("update", ended[count], count)]


def shards(order, stages, schur_matrix, newton_rhs):
    row_count, col_count = lax.axis_size("row"), lax.axis_size("col")
    own_row, own_col = lax.axis_index("row"), lax.axis_index("col")
    local_rows, _ = schur_matrix.shape
    depth = col_count // 2
    line, side = own_col // 2, own_col % 2
    count, half = local_rows // NB, NB // 2
    last = max(at for at, _, _ in stages)
    mid = stages[0][2]

    def link(value, *pairs):
        return lax.ppermute(value, "col", [(a * 2 + i, b * 2 + j) for (a, i), (b, j) in pairs])

    def down(value, row):
        above = parent(row)
        if row - above > 1:
            return lax.ppermute(value, "row", [(above, row)])
        return lax.ppermute(value, "row", [(at, at ^ 1) for at in range(row_count)])

    def choose(options):
        return jnp.where(place[2] == 0, options[0], jnp.where(place[2] == 1, options[1], jnp.where(side == 0, options[2], options[3])))

    def cut(source, low, high):
        return list(lax.optimization_barrier([source[at * half : (at + 1) * half, :NB] for at in range(low, high)]))

    pieces = cut(schur_matrix, 0, 4)
    later = barrier(schur_matrix, pieces)
    pieces += cut(later, 4, 8)
    later = barrier(later, pieces[4:])
    strip = lax.optimization_barrier(later[:NB, :])
    pieces += cut(barrier(later, [strip]), 8, 2 * count)
    place = jnp.stack([own_row, own_col, jnp.where(own_col < 2, own_col, 2 + side)]).astype(jnp.int32)
    rhs = newton_rhs.reshape(1, local_rows)

    sides = {at: [i for i, ok in ((0, at < count), (1, at > 0)) if ok] for at in range(count + 1)}
    sources = {b: (a, stage) for stage, a, b in stages}
    first, lower, onward, spread, crossed, closed = {}, {}, {}, {}, {}, {}
    columns, panels, strips, pivots, factors, done = {}, {}, {0: strip}, {}, None, ()

    def column(pair, stage):
        if (pair, stage) not in columns:
            if stage == 1:
                a, b = onward.get(pair - 1), lower.get(pair)
                columns[pair, 1] = b if a is None else a if b is None else jnp.where(side == 0, b, a)
            else:
                value = column(pair, stage - 1)
                for s, _, b in stages:
                    if s == stage - 1:
                        value = jnp.where(line == b, spread[pair, b], value)
                columns[pair, stage] = value
        return columns[pair, stage]

    def panel(section):
        if section not in panels:
            own = barrier(schur_matrix, [closed[section]])[section * NB : (section + 1) * NB, :NB]
            upper = [own[:half], first[section], crossed[section + 1], column(section + 1, last + 1)]
            under = [own[half:], closed[section], column(section, last + 1), crossed[section]]
            panels[section] = jnp.concatenate([choose(upper), choose(under)])
        return panels[section]

    for step in order:
        name, at = step[:2]
        if name == "pivot" and 0 not in pivots:
            pivots[0] = jnp.concatenate([panel(0), jnp.broadcast_to(newton_rhs[None, :NB], (8, NB))])
        if name == "solve":
            block = pivots[0]
            for row in range(1, row_count):
                block = jnp.where(own_row == row, pivots[row], block)
        if name == "first":
            first[at] = link(pieces[2 * at], ((0, 0), (0, 1)))
        elif name == "lower":
            lower[at] = link(pieces[2 * at + 1], ((0, 0), (mid, 0)))
        elif name == "onward":
            onward[at] = link(first[at], ((0, 1), (mid, 1)))
        elif name == "spread":
            source, stage = sources[step[2]]
            spread[at, step[2]] = link(column(at, stage), *[((source, i), (step[2], i)) for i in sides[at]])
        elif name == "cross":
            crossed[at] = link(column(at, last + 1), *[((k, i), (k, 1 - i)) for k in range(1, depth) for i in sides[at]])
        elif name == "close":
            closed[at] = link(crossed[at], ((1, 1), (0, 1)))
        elif name == "strip":
            strips[at] = down(strips[parent(at)], at)
        elif name == "pivot":
            pivots[at] = down(pivots[parent(at)], at)
        elif name == "solve":
            factors = solve(place, block, schur_matrix, [strips[row] for row in range(1, row_count)])
        else:
            group = [panel(section) for section in range(at, step[2])]
            if at == 0:
                group[0] = jnp.where(own_row == 0, 0.0, group[0])
            done = update(at, schur_matrix, rhs, factors, group, done)
    return done[0], done[1].reshape(local_rows)


def solution(mesh):
    row_count, col_count = mesh.shape["row"], mesh.shape["col"]
    stages = fan_out(0, 1, col_count // 2)

    def program(schur_matrix, newton_rhs):
        order = plan(schur_matrix.shape[0] // row_count // NB, stages, row_count)

        def body(*args):
            return shards(order, stages, *args)

        step = jax.shard_map(
            body,
            mesh=mesh,
            in_specs=(P("row", "col"), P("row")),
            out_specs=(P("row", "col"), P("row")),
            check_vma=False,
        )
        return step(schur_matrix, newton_rhs)

    return program
```
